128 devices in a mesh: dp: 16 (over z, y), mp: 8 (over x, core).
Axes of the slice: x: 4, y: 4, z: 4, core: 2. Of those that a mesh axis runs over, the one named last changes fastest.
Arguments:
- cotangent: bfloat16 [32768, 4096], P('dp'), may hold values from -64 to 64, as said below
- activation: bfloat16 [32768, 8192], P('dp', 'mp'), may hold values from -64 to 64, as said below
Outputs:
- update: bfloat16 [4096, 8192], P('dp', 'mp')
The draws below stay inside these ranges and needn't reach their ends.
Inputs may be any that keep to these rules, and one draw needn't show every extreme that they name: `cotangent`: real-valued entries. `activation`: real-valued entries.
All inputs are finite; a program needn't handle non-finite values.
Results may differ from the reference program's by a relative error of at most 0.0054.
Values may be sent and summed in bfloat16 or wider, within the bound.
A program may use at most 256 MiB of HBM per device.

```python
import math
import jax
import jax.numpy as jnp
from jax import lax

N = 8192
ROWS = 4096
TOKENS = 32768


def feature_field(key, width, salt):
    noise = jax.random.normal(jax.random.fold_in(key, salt), (TOKENS, width), jnp.float32)
    spread = math.log(4.0)
    ramp = jnp.exp(math.log(3.0) * jnp.arange(width, dtype=jnp.float32) / max(width - 1, 1))
    rough = jnp.exp(jax.random.uniform(jax.random.fold_in(key, salt + 2), (width,), jnp.float32, 0.0, spread))
    return jnp.clip(noise * (ramp * rough)[None, :], -64.0, 64.0)


def draw_cotangent(key, part):
    return feature_field(key, ROWS, 10).astype(jnp.bfloat16)


def draw_activation(key, part):
    return feature_field(key, N, 20).astype(jnp.bfloat16)


def setup_inputs(seed: int = 0) -> dict:
    streams_of = jax.random.split(jax.random.key(seed), 3)
    return {
        "cotangent": draw_cotangent(jax.random.fold_in(streams_of[2], 71), 0),
        "activation": draw_activation(jax.random.fold_in(streams_of[2], 71), 0),
    }


LINEAR_COEF = 3.4445
CUBIC_COEF = -4.775
QUINTIC_COEF = 2.0315
NORM_EPSILON = 1e-07
NORM_SHARE = 0.25

def reference(cotangent, activation):
    dy_full = cotangent.astype(jnp.float32)
    act_full = activation.astype(jnp.float32)
    gradient = lax.dot_general(dy_full, act_full, (((0,), (0,)), ((), ())), preferred_element_type=jnp.float32)
    sum_squares = jnp.sum(gradient * gradient)
    factor = NORM_SHARE * math.sqrt(ROWS) / (jnp.sqrt(sum_squares) + NORM_EPSILON)
    normalized = (gradient * factor).astype(jnp.bfloat16)
    normal_wide = normalized.astype(jnp.float32)
    gram = jnp.dot(normal_wide, normal_wide.T, preferred_element_type=jnp.float32).astype(jnp.bfloat16)
    gram_wide = gram.astype(jnp.float32)
    square = jnp.dot(gram_wide, gram_wide, preferred_element_type=jnp.float32)
    polynomial = (CUBIC_COEF * gram_wide + QUINTIC_COEF * square).astype(jnp.bfloat16)
    mixed = jnp.dot(polynomial.astype(jnp.float32), normal_wide, preferred_element_type=jnp.float32)
    rescale = math.sqrt(N)
    return (rescale * (LINEAR_COEF * normal_wide + mixed)).astype(jnp.bfloat16)
```

```python
import math

import jax
import jax.numpy as jnp
from jax import lax
from jax.experimental import pallas as pl
from jax.experimental.pallas import tpu as pltpu
from jax.sharding import PartitionSpec as P

N = 8192
ROWS = 4096

LINEAR_COEF = 3.4445
CUBIC_COEF = -4.775
QUINTIC_COEF = 2.0315
NORM_EPSILON = 1e-07
NORM_SHARE = 0.25

BF = jnp.bfloat16
F32 = jnp.float32
NN = (((1,), (0,)), ((), ()))
NT = (((1,), (1,)), ((), ()))
SHIFT = (0, 1, 3, 2)
PLUS, MINUS = 0, 1


def dot(a, b, dims=NN):
    return lax.dot_general(a, b, dims, preferred_element_type=F32)


def kernel(
    c_ref, a_ref, out_ref,
    a_t, a_in, c_in, a_sem, c_sem,
    far_out, far_in, near_out, near_in, via_out, via_in, via_sum, own_sum, g_send, g_recv,
    rs_far_out, rs_far_in, rs_near_out, rs_near_in, rs_via_out, rs_via_in, rs_via, rs_own, rs_send, rs_recv,
    grad, z_group, y_group, ag_send, ag_recv,
    tile, half_out, half_in, pair_send, pair_recv,
    x_far_out, x_far_in, x_near_out, x_near_in, x_via_out, x_via_in, x_send, x_recv,
    gram, gx_send, gx_recv, gp_send, gp_recv,
    values, sq, sq_send, sq_recv,
):
    dp, mp = lax.axis_index("dp"), lax.axis_index("mp")
    z, y = dp // 4, lax.rem(dp, 4)
    x, core = mp // 2, lax.rem(mp, 2)

    def at(axis, step):
        if axis == "z":
            return (lax.rem(z + step, 4) * 4 + y, mp)
        if axis == "y":
            return (z * 4 + lax.rem(y + step, 4), mp)
        if axis == "x":
            return (dp, lax.rem(x + step, 4) * 2 + core)
        return (dp, x * 2 + 1 - core)

    STEP = (1, 3)
    sent = []

    def copy(src, dst, send, recv, axis, direction):
        return pltpu.make_async_remote_copy(
            src_ref=src, dst_ref=dst, send_sem=send, recv_sem=recv,
            device_id=at(axis, STEP[direction]), device_id_type=pl.DeviceIdType.MESH,
        )

    def send(*args):
        c = copy(*args)
        c.start()
        sent.append(c)
        return c

    def load_a(q):
        return pltpu.make_async_copy(a_ref.at[:, pl.ds(q * 256, 256)], a_in.at[q % 2], a_sem.at[q % 2])

    def pick(k):
        return jnp.where(k == 0, 2, jnp.where(k == 1, 1, jnp.where(k == 2, 3, 0)))

    def block(u):
        first = u < 8
        last = u >= 24
        v = jnp.where(first, u, jnp.where(last, u - 24, u - 8))
        pairs = first | last
        k = jnp.where(pairs, v // 2, v // 4)
        h = jnp.where(pairs, lax.rem(v, 2), lax.rem(v // 2, 2))
        d = lax.rem(v, 2)
        step = jnp.where(first, 2, jnp.where(last, 0, 1 + 2 * d))
        one = jnp.where(h == 0, z, y)
        two = jnp.where(h == 0, y, z)
        one = lax.rem(one + step, 4)
        two = lax.rem(two + pick(k), 4)
        return jnp.where(h == 0, one * 4 + two, two * 4 + one)

    def load_c(u):
        slot = lax.rem(u, 4)
        col = pl.multiple_of(block(u) * 256, 256)
        return pltpu.make_async_copy(c_ref.at[:, pl.ds(col, 256)], c_in.at[slot], c_sem.at[slot])

    load_a(0).start()
    load_a(1).start()
    for u in range(3):
        load_c(jnp.int32(u)).start()

    barrier = pltpu.get_barrier_semaphore()
    for axis in ("z", "y", "x"):
        for step in (1, 2, 3):
            pl.semaphore_signal(barrier, inc=1, device_id=at(axis, step), device_id_type=pl.DeviceIdType.MESH)
    pl.semaphore_signal(barrier, inc=1, device_id=at("core", 0), device_id_type=pl.DeviceIdType.MESH)

    for q in range(4):
        load_a(q).wait()
        a_t[pl.ds(q * 256, 256), :] = a_in[q % 2].T
        if q < 2:
            load_a(q + 2).start()
    pl.semaphore_wait(barrier, 10)

    AXIS1 = ("z", "y")
    AXIS2 = ("y", "z")

    def unit(h, u):
        @pl.when(u + 3 < 32)
        def _():
            load_c(u + 3).start()

        load_c(u).wait()
        return dot(a_t[pl.ds(h * 512, 512), :], c_in[lax.rem(u, 4)])

    def far_copy(h, d, k):
        return copy(far_out.at[h, k, pl.ds(d * 256, 256)], far_in.at[h, d, k],
                    g_send.at[0, h, d, k], g_recv.at[0, h, d, k], AXIS1[h], d)

    def near_copy(h, d, k):
        return copy(near_out.at[h, d, k], near_in.at[h, d, k],
                    g_send.at[1, h, d, k], g_recv.at[1, h, d, k], AXIS1[h], d)

    def via_copy(h, d, k):
        return copy(via_out.at[h, d, k], via_in.at[h, d, k],
                    g_send.at[2, h, d, k], g_recv.at[2, h, d, k], AXIS1[h], d)

    def far_body(k, carry):
        for h in range(2):
            far_out[h, k] = unit(h, 2 * k + h).astype(BF)
            for d in range(2):
                far_copy(h, d, k).start()
        return carry

    def near_body(k, carry):
        for h in range(2):
            for d in range(2):
                r = unit(h, 8 + 4 * k + 2 * h + d)
                direct, relayed = 1 - d, d
                near_out[h, d, k] = r[direct * 256:direct * 256 + 256].astype(BF)
                via_sum[h, d, k] = r[relayed * 256:relayed * 256 + 256]
                near_copy(h, d, k).start()
        return carry

    def via_body(k, carry):
        for h in range(2):
            for d in range(2):
                far_copy(h, d, k).wait_recv()
                via_out[h, d, k] = (via_sum[h, d, k] + far_in[h, d, k].astype(F32)).astype(BF)
                via_copy(h, d, k).start()
        return carry

    def own_body(k, carry):
        for h in range(2):
            own_sum[h, k] = unit(h, 24 + 2 * k + h)
        return carry

    lax.fori_loop(0, 4, far_body, 0)
    lax.fori_loop(0, 4, near_body, 0)
    lax.fori_loop(0, 4, via_body, 0)
    lax.fori_loop(0, 4, own_body, 0)

    def first_sum(h, k):
        for d in range(2):
            near_copy(h, d, k).wait_recv()
            via_copy(h, d, k).wait_recv()
        top = own_sum[h, k, 0:256] + via_in[h, 0, k].astype(F32) + near_in[h, 1, k].astype(F32)
        low = own_sum[h, k, 256:512] + near_in[h, 0, k].astype(F32) + via_in[h, 1, k].astype(F32)
        return top, low

    def rs_copy(n, h, kind, d, axis):
        src, dst = (
            (rs_far_out.at[n, h, pl.ds(d * 256, 256)], rs_far_in.at[n, h, d]),
            (rs_near_out.at[n, h, d], rs_near_in.at[n, h, d]),
            (rs_via_out.at[n, h, d], rs_via_in.at[n, h, d]),
        )[kind]
        return src, dst, rs_send.at[n, h, kind, d], rs_recv.at[n, h, kind, d], axis, d

    def rs_put(n, h, axis, slot, top, low):
        if slot == 3:
            rs_far_out[n, h, 0:256] = top.astype(BF)
            rs_far_out[n, h, 256:512] = low.astype(BF)
            for d in range(2):
                send(*rs_copy(n, h, 0, d, axis))
        elif slot == 1:
            rs_near_out[n, h, 0] = low.astype(BF)
            send(*rs_copy(n, h, 1, 0, axis))
            rs_via[h, 0] = top
        elif slot == 2:
            rs_near_out[n, h, 1] = top.astype(BF)
            send(*rs_copy(n, h, 1, 1, axis))
            rs_via[h, 1] = low
        else:
            rs_own[h, 0:256] = top
            rs_own[h, 256:512] = low

    def rs_relay(n, h, axis):
        for d in range(2):
            copy(*rs_copy(n, h, 0, d, axis)).wait_recv()
            rs_via_out[n, h, d] = (rs_via[h, d] + rs_far_in[n, h, d].astype(F32)).astype(BF)
            send(*rs_copy(n, h, 2, d, axis))

    def rs_finish(n, h, axis):
        for kind in (1, 2):
            for d in range(2):
                copy(*rs_copy(n, h, kind, d, axis)).wait_recv()
        top = rs_own[h, 0:256] + rs_via_in[n, h, 0].astype(F32) + rs_near_in[n, h, 1].astype(F32)
        low = rs_own[h, 256:512] + rs_near_in[n, h, 0].astype(F32) + rs_via_in[n, h, 1].astype(F32)
        return top, low

    def ag_copy(n, buf, rows, kind, d, axis):
        part = d if kind in (0, 2) else 1 - d
        there = (2, 1)[d]
        here, target = (0, there) if kind < 2 else (there, 3)
        r = pl.ds(part * rows, rows)
        return (buf.at[r, pl.ds(here * 256, 256)], buf.at[r, pl.ds(target * 256, 256)],
                ag_send.at[n, kind, d], ag_recv.at[n, kind, d], axis, d)

    def ag_own(n, buf, rows, axis, part):
        for d in range(2):
            send(*ag_copy(n, buf, rows, 0 if d == part else 1, d, axis))

    def ag_relay(n, buf, rows, axis):
        for d in range(2):
            copy(*ag_copy(n, buf, rows, 0, d, axis)).wait_recv()
            send(*ag_copy(n, buf, rows, 2, d, axis))

    def ag_near(n, buf, rows, axis):
        for d in range(2):
            copy(*ag_copy(n, buf, rows, 1, d, axis)).wait_recv()

    def ag_far(n, buf, rows, axis):
        for d in range(2):
            copy(*ag_copy(n, buf, rows, 2, d, axis)).wait_recv()

    for k, slot in ((0, 3), (1, 1), (2, 2)):
        for h in range(2):
            top, low = first_sum(h, k)
            rs_put(0, h, AXIS2[h], slot, top, low)
    for h in range(2):
        rs_relay(0, h, AXIS2[h])
    for h in range(2):
        top, low = first_sum(h, 3)
        rs_put(0, h, AXIS2[h], 0, top, low)

    squares = jnp.zeros((1, 256), F32)
    for h in range(2):
        top, low = rs_finish(0, h, AXIS2[h])
        grad[h, 0:256] = top
        grad[h, 256:512] = low
        for part, value in ((0, top), (1, low)):
            r = pl.ds(h * 512 + part * 256, 256)
            z_group[r, 0:256] = value.astype(BF)
            y_group[r, 0:256] = value.astype(BF)
            squares += jnp.sum(value * value, axis=0, keepdims=True)
        ag_own(0, z_group, 512, "y", h)
        ag_own(1, y_group, 512, "z", h)

    def sq_copies(n, axis):
        if axis == "core":
            steps = (1,)
        else:
            steps = (1, 2, 3)
        return [
            pltpu.make_async_remote_copy(
                src_ref=sq.at[n, 0], dst_ref=sq.at[n, step],
                send_sem=sq_send.at[n, step], recv_sem=sq_recv.at[n, step],
                device_id=at(axis, step), device_id_type=pl.DeviceIdType.MESH,
            )
            for step in steps
        ]

    def sq_start(n, axis, value):
        sq[n, 0] = jnp.broadcast_to(value, (8, 256))
        for c in sq_copies(n, axis):
            c.start()
            sent.append(c)

    def sq_total(n, axis):
        total = sq[n, 0]
        for step, c in enumerate(sq_copies(n, axis)):
            c.wait_recv()
            total += sq[n, step + 1]
        return total

    sq_start(0, "z", squares)

    ag_relay(0, z_group, 512, "y")
    ag_relay(1, y_group, 512, "z")
    ag_near(0, z_group, 512, "y")
    ag_near(1, y_group, 512, "z")

    def turn(slot):
        a_t[pl.ds(slot * 256, 256), 0:1024] = z_group[:, slot * 256:slot * 256 + 256].T

    for slot in range(3):
        turn(slot)
    sq_start(1, "y", sq_total(0, "z"))
    ag_far(0, z_group, 512, "y")
    ag_far(1, y_group, 512, "z")
    turn(3)

    mine = pl.multiple_of(core * 512, 512)
    other = pl.multiple_of((1 - core) * 512, 512)

    def half_copy(step):
        r = pl.ds(pl.multiple_of(lax.rem(x + step, 4) * 128, 128), 128)
        return half_out.at[r], half_in.at[r], pair_send.at[step], pair_recv.at[step], "core", 0

    def other_body(i, carry):
        cols = pl.ds(pl.multiple_of(i * 256, 256), 256)
        half_out[:, cols] = dot(a_t[pl.ds(other, 512), 0:1024], y_group[:, cols]).astype(BF)
        return carry

    def mine_body(i, carry):
        cols = pl.ds(pl.multiple_of(i * 256, 256), 256)
        tile[:, cols] = dot(a_t[pl.ds(mine, 512), 0:1024], y_group[:, cols])
        return carry

    lax.fori_loop(0, 4, other_body, 0)
    for step in (2, 1, 3, 0):
        send(*half_copy(step))
    lax.fori_loop(0, 4, mine_body, 0)
    sq_start(2, "x", sq_total(1, "y"))

    def pair_sum(step):
        copy(*half_copy(step)).wait_recv()
        r = pl.ds(pl.multiple_of(lax.rem(x + step, 4) * 128, 128), 128)
        return tile[r, :] + half_in[r, :].astype(F32)

    def x_copy(kind, d):
        src, dst = (
            (x_far_out.at[d], x_far_in.at[d]),
            (x_near_out.at[d], x_near_in.at[d]),
            (x_via_out.at[d], x_via_in.at[d]),
        )[kind]
        return src, dst, x_send.at[kind, d], x_recv.at[kind, d], "x", d

    s = pair_sum(2)
    for d in range(2):
        x_far_out[d] = s[:, d * 512:d * 512 + 512].astype(BF)
        send(*x_copy(0, d))
    relayed = []
    for d in range(2):
        s = pair_sum(STEP[d])
        x_near_out[d] = s[:, (1 - d) * 512:(1 - d) * 512 + 512].astype(BF)
        send(*x_copy(1, d))
        r = pl.ds(pl.multiple_of(lax.rem(x + STEP[d], 4) * 128, 128), 128)
        tile[r, d * 512:d * 512 + 512] = s[:, d * 512:d * 512 + 512]
    s = pair_sum(0)
    here = pl.ds(pl.multiple_of(x * 128, 128), 128)
    tile[here, :] = s
    for d in range(2):
        copy(*x_copy(0, d)).wait_recv()
        r = pl.ds(pl.multiple_of(lax.rem(x + STEP[d], 4) * 128, 128), 128)
        x_via_out[d] = (tile[r, d * 512:d * 512 + 512] + x_far_in[d].astype(F32)).astype(BF)
        send(*x_copy(2, d))
    for kind in (1, 2):
        for d in range(2):
            copy(*x_copy(kind, d)).wait_recv()

    def chunk(step, part):
        r = pl.ds(pl.multiple_of(core * 512 + lax.rem(x + step, 4) * 128, 128), 128)
        return gram.at[r, pl.ds(part * 512, 512)]

    chunk(0, 0)[...] = (
        tile[here, 0:512] + x_via_in[0].astype(F32) + x_near_in[1].astype(F32)
    ).astype(BF)
    chunk(0, 1)[...] = (
        tile[here, 512:1024] + x_near_in[0].astype(F32) + x_via_in[1].astype(F32)
    ).astype(BF)

    def gx_copy(kind, d):
        part = d if kind in (0, 2) else 1 - d
        step = 0 if kind < 2 else STEP[1 - d]
        return chunk(step, part), chunk(step, part), gx_send.at[kind, d], gx_recv.at[kind, d], "x", d

    def gx_arrived(kind, d):
        part = d if kind in (0, 2) else 1 - d
        step = STEP[1 - d] if kind < 2 else 2
        ref = chunk(step, part)
        copy(ref, ref, gx_send.at[kind, d], gx_recv.at[kind, d], "x", d).wait_recv()
        return step, part

    def gp_copy(step, part):
        ref = chunk(step, part)
        return ref, ref, gp_send.at[step, part], gp_recv.at[step, part], "core", 0

    for kind in (0, 1):
        for d in range(2):
            send(*gx_copy(kind, d))
    for part in range(2):
        send(*gp_copy(0, part))
    sq_start(3, "core", sq_total(2, "x"))
    arrived = []
    for d in range(2):
        arrived.append(gx_arrived(0, d))
        send(*gx_copy(2, d))
    for d in range(2):
        send(*gp_copy(*arrived[d]))
    for kind in (1, 2):
        for d in range(2):
            send(*gp_copy(*gx_arrived(kind, d)))
    for step in range(4):
        for part in range(2):
            r = pl.ds(pl.multiple_of((1 - core) * 512 + lax.rem(x + step, 4) * 128, 128), 128)
            ref = gram.at[r, pl.ds(part * 512, 512)]
            copy(ref, ref, gp_send.at[step, part], gp_recv.at[step, part], "core", 0).wait_recv()

    total = jnp.sum(sq_total(3, "core")[0:1, :], axis=1, keepdims=True)
    factor = NORM_SHARE * math.sqrt(ROWS) / (jnp.sqrt(total) + NORM_EPSILON)

    def down(lhs, slot):
        return dot(lhs, gram[:, slot * 256:slot * 256 + 256])

    def across(lhs, slot):
        return dot(lhs, gram[slot * 256:slot * 256 + 256, :], NT)

    for slot in (3, 1, 2, 0):
        w = down(z_group[0:512, :], slot)
        rs_put(1, 0, "z", slot, w[0:256], w[256:512])
        w = across(y_group[512:1024, :], slot)
        rs_put(1, 1, "y", slot, w[0:256], w[256:512])
    for h in range(2):
        rs_relay(1, h, AXIS1[h])
    for h in range(2):
        for part, w in enumerate(rs_finish(1, h, AXIS1[h])):
            r = pl.ds(part * 256, 256)
            v = CUBIC_COEF * grad[h, r] + (QUINTIC_COEF * factor * factor) * w
            values[h, r, 0:256] = v.astype(BF)
            ag_own(2 + h, values.at[h], 256, AXIS1[h], part)
    for h in range(2):
        ag_relay(2 + h, values.at[h], 256, AXIS1[h])
    for h in range(2):
        ag_near(2 + h, values.at[h], 256, AXIS1[h])
        ag_far(2 + h, values.at[h], 256, AXIS1[h])
    for slot in (3, 1, 2, 0):
        m = across(values[0], slot)
        rs_put(2, 0, "y", slot, m[0:256], m[256:512])
        m = down(values[1], slot)
        rs_put(2, 1, "z", slot, m[0:256], m[256:512])
    for h in range(2):
        rs_relay(2, h, AXIS2[h])
    scale = math.sqrt(N) * factor
    for h in range(2):
        for part, m in enumerate(rs_finish(2, h, AXIS2[h])):
            r = pl.ds(part * 256, 256)
            o = scale * (LINEAR_COEF * grad[h, r] + (factor * factor) * m)
            out_ref[:, h * 512 + part * 256:h * 512 + part * 256 + 256] = o.T.astype(BF)

    def drain(k, carry):
        for h in range(2):
            for d in range(2):
                far_copy(h, d, k).wait_send()
                near_copy(h, d, k).wait_send()
                via_copy(h, d, k).wait_send()
        return carry

    lax.fori_loop(0, 4, drain, 0)
    for c in sent:
        c.wait_send()


def local(cotangent, activation):
    dma = pltpu.SemaphoreType.DMA
    vm = pltpu.VMEM
    piece = (256, 256)
    return pl.pallas_call(
        kernel,
        out_shape=jax.ShapeDtypeStruct((256, 1024), BF),
        in_specs=[pl.BlockSpec(memory_space=pl.ANY)] * 2,
        out_specs=pl.BlockSpec(memory_space=pltpu.VMEM),
        scratch_shapes=[
            vm((1024, 2048), BF), vm((2, 2048, 256), BF), vm((4, 2048, 256), BF), dma((2,)), dma((4,)),
            vm((2, 4, 512, 256), BF), vm((2, 2, 4) + piece, BF),
            vm((2, 2, 4) + piece, BF), vm((2, 2, 4) + piece, BF),
            vm((2, 2, 4) + piece, BF), vm((2, 2, 4) + piece, BF),
            vm((2, 2, 4) + piece, F32), vm((2, 4, 512, 256), F32),
            dma((3, 2, 2, 4)), dma((3, 2, 2, 4)),
            vm((3, 2, 512, 256), BF), vm((3, 2, 2) + piece, BF),
            vm((3, 2, 2) + piece, BF), vm((3, 2, 2) + piece, BF),
            vm((3, 2, 2) + piece, BF), vm((3, 2, 2) + piece, BF),
            vm((2, 2) + piece, F32), vm((2, 512, 256), F32),
            dma((3, 2, 3, 2)), dma((3, 2, 3, 2)),
            vm((2, 512, 256), F32), vm((1024, 1024), BF), vm((1024, 1024), BF), dma((4, 3, 2)), dma((4, 3, 2)),
            vm((512, 1024), F32), vm((512, 1024), BF), vm((512, 1024), BF), dma((4,)), dma((4,)),
            vm((2, 128, 512), BF), vm((2, 128, 512), BF), vm((2, 128, 512), BF),
            vm((2, 128, 512), BF), vm((2, 128, 512), BF), vm((2, 128, 512), BF), dma((3, 2)), dma((3, 2)),
            vm((1024, 1024), BF), dma((3, 2)), dma((3, 2)), dma((4, 2)), dma((4, 2)),
            vm((2, 512, 1024), BF), vm((4, 4, 8, 256), F32), dma((4, 4)), dma((4, 4)),
        ],
        compiler_params=pltpu.CompilerParams(
            collective_id=0, has_side_effects=True, vmem_limit_bytes=67043328
        ),
        name="muon_step",
    )(cotangent, activation)


def solution(mesh):
    return jax.shard_map(
        local,
        mesh=mesh,
        in_specs=(P("dp", None), P("dp", "mp")),
        out_specs=P("dp", "mp"),
        check_vma=False,
    )
```

```python
import math

import jax
import jax.numpy as jnp
from jax import lax
from jax.experimental import pallas as pl
from jax.experimental.pallas import tpu as pltpu
from jax.sharding import PartitionSpec as P

N = 8192
ROWS = 4096

LINEAR_COEF = 3.4445
CUBIC_COEF = -4.775
QUINTIC_COEF = 2.0315
NORM_EPSILON = 1e-07
NORM_SHARE = 0.25

BF = jnp.bfloat16
F32 = jnp.float32
NN = (((1,), (0,)), ((), ()))
NT = (((1,), (1,)), ((), ()))
FIRST_USE = ((2, 2), (2, 1), (1, 2), (2, 3), (3, 2), (2, 0), (0, 2), (1, 1), (3, 1), (1, 3), (3, 3), (1, 0), (3, 0), (0, 1), (0, 3), (0, 0))
LATE = FIRST_USE[12:]
PLUS, MINUS = 0, 1


def dot(a, b, dims=NN):
    return lax.dot_general(a, b, dims, preferred_element_type=F32)


def kernel(
    c_ref, a_ref, out_ref,
    a_t, c_in, a_sem, c_sem,
    far_out, far_in, near_out, near_in, via_out, via_in, via_sum, own_sum, g_send, g_recv,
    rs_far_out, rs_far_in, rs_near_out, rs_near_in, rs_via_out, rs_via_in, rs_send, rs_recv,
    grad, z_group, y_group, ag_send, ag_recv,
    half_in, pair_send, pair_recv,
    x_far_out, x_far_in, x_near_out, x_near_in, x_via_out, x_via_in, x_send, x_recv,
    gram, gx_send, gx_recv, gp_send, gp_recv,
    values, sq, sq_send, sq_recv,
):
    dp, mp = lax.axis_index("dp"), lax.axis_index("mp")
    z, y = dp // 4, lax.rem(dp, 4)
    x, core = mp // 2, lax.rem(mp, 2)

    def at(axis, step):
        if axis == "z":
            return (lax.rem(z + step, 4) * 4 + y, mp)
        if axis == "y":
            return (z * 4 + lax.rem(y + step, 4), mp)
        if axis == "x":
            return (dp, lax.rem(x + step, 4) * 2 + core)
        return (dp, x * 2 + 1 - core)

    STEP = (1, 3)
    sent = []

    def copy(src, dst, send, recv, axis, direction):
        return pltpu.make_async_remote_copy(
            src_ref=src, dst_ref=dst, send_sem=send, recv_sem=recv,
            device_id=at(axis, STEP[direction]), device_id_type=pl.DeviceIdType.MESH,
        )

    def send(*args):
        c = copy(*args)
        c.start()
        sent.append(c)
        return c

    tile = via_sum.at[0:512]
    half_out = a_t.at[0:512, 1024:2048]
    rs_own = own_sum.at[:, 1]

    def load_a(q):
        slot = 4 * LATE[q][0] + LATE[q][1]
        return pltpu.make_async_copy(a_ref.at[:, pl.ds(q * 256, 256)], c_in.at[slot], a_sem.at[q])

    def pick(k):
        return jnp.where(k == 0, 2, jnp.where(k == 1, 1, jnp.where(k == 2, 3, 0)))

    def load_c(dz, dy):
        slot = 4 * dz + dy
        col = pl.multiple_of((4 * lax.rem(z + dz, 4) + lax.rem(y + dy, 4)) * 256, 256)
        return pltpu.make_async_copy(c_ref.at[:, pl.ds(col, 256)], c_in.at[slot], c_sem.at[slot])

    for q in range(4):
        load_a(q).start()
    for dz, dy in FIRST_USE[:12]:
        load_c(dz, dy).start()

    barrier = pltpu.get_barrier_semaphore()
    for axis in ("z", "y", "x"):
        for step in (1, 2, 3):
            pl.semaphore_signal(barrier, inc=1, device_id=at(axis, step), device_id_type=pl.DeviceIdType.MESH)
    pl.semaphore_signal(barrier, inc=1, device_id=at("core", 0), device_id_type=pl.DeviceIdType.MESH)

    for q in range(4):
        load_a(q).wait()
        a_t[pl.ds(q * 256, 256), :] = c_in[4 * LATE[q][0] + LATE[q][1]].T
        load_c(*LATE[q]).start()
    pl.semaphore_wait(barrier, 10)

    AXIS1 = ("z", "y")
    AXIS2 = ("y", "z")

    def unit(h, step, k):
        slot = 4 * step + pick(k) if h == 0 else 4 * pick(k) + step
        return dot(a_t[pl.ds(h * 512, 512), :], c_in[slot])

    def far_copy(h, d, k):
        return copy(far_out.at[h, k, pl.ds(d * 256, 256)], far_in.at[h, d, k],
                    g_send.at[0, h, d, k], g_recv.at[0, h, d, k], AXIS1[h], d)

    def near_copy(h, d, k):
        return copy(near_out.at[h, d, k], near_in.at[h, d, k],
                    g_send.at[1, h, d, k], g_recv.at[1, h, d, k], AXIS1[h], d)

    def via_copy(h, d, k):
        return copy(via_out.at[h, d, k], via_in.at[h, d, k],
                    g_send.at[2, h, d, k], g_recv.at[2, h, d, k], AXIS1[h], d)

    def far_body(k, carry):
        load_c(2, pick(k)).wait()

        @pl.when(k > 0)
        def _():
            load_c(pick(k), 2).wait()

        for h in range(2):
            far_out[h, k] = unit(h, 2, k).astype(BF)
            for d in range(2):
                far_copy(h, d, k).start()
        return carry

    def piece(h, d, k):
        return pl.ds((2 * h + d) * 256, 256), pl.ds(pl.multiple_of(k * 256, 256), 256)

    def near_body(k, carry):
        for when, blocks in ((1, FIRST_USE[7:10]), (2, FIRST_USE[10:11]), (3, FIRST_USE[11:15])):
            @pl.when(k == when)
            def _():
                for dz, dy in blocks:
                    load_c(dz, dy).wait()

        for h in range(2):
            for d in range(2):
                r = unit(h, 1 + 2 * d, k)
                direct, relayed = 1 - d, d
                near_out[h, d, k] = r[direct * 256:direct * 256 + 256].astype(BF)
                via_sum[piece(h, d, k)] = r[relayed * 256:relayed * 256 + 256]
                near_copy(h, d, k).start()
        return carry

    def via_body(k, carry):
        for h in range(2):
            for d in range(2):
                far_copy(h, d, k).wait_recv()
                via_out[h, d, k] = (via_sum[piece(h, d, k)] + far_in[h, d, k].astype(F32)).astype(BF)
                via_copy(h, d, k).start()
        return carry

    def own_body(k, carry):
        @pl.when(k == 3)
        def _():
            load_c(0, 0).wait()

        for h in range(2):
            own_sum[h, k] = unit(h, 0, k)
        return carry

    lax.fori_loop(0, 4, far_body, 0)
    lax.fori_loop(0, 4, near_body, 0)
    lax.fori_loop(0, 4, via_body, 0)
    lax.fori_loop(0, 4, own_body, 0)

    def first_sum(h, k):
        for d in range(2):
            near_copy(h, d, k).wait_recv()
            via_copy(h, d, k).wait_recv()
        top = own_sum[h, k, 0:256] + via_in[h, 0, k].astype(F32) + near_in[h, 1, k].astype(F32)
        low = own_sum[h, k, 256:512] + near_in[h, 0, k].astype(F32) + via_in[h, 1, k].astype(F32)
        return top, low

    def rs_copy(n, h, kind, d, axis):
        src, dst = (
            (rs_far_out.at[n, h, pl.ds(d * 256, 256)], rs_far_in.at[n, h, d]),
            (rs_near_out.at[n, h, d], rs_near_in.at[n, h, d]),
            (rs_via_out.at[n, h, d], rs_via_in.at[n, h, d]),
        )[kind]
        return src, dst, rs_send.at[n, h, kind, d], rs_recv.at[n, h, kind, d], axis, d

    def rs_put(n, h, axis, slot, top, low):
        if slot == 3:
            rs_far_out[n, h, 0:256] = top.astype(BF)
            rs_far_out[n, h, 256:512] = low.astype(BF)
            for d in range(2):
                send(*rs_copy(n, h, 0, d, axis))
        elif slot == 1:
            rs_near_out[n, h, 0] = low.astype(BF)
            send(*rs_copy(n, h, 1, 0, axis))
            own_sum[h, 0, 0:256] = top
        elif slot == 2:
            rs_near_out[n, h, 1] = top.astype(BF)
            send(*rs_copy(n, h, 1, 1, axis))
            own_sum[h, 0, 256:512] = low
        else:
            rs_own[h, 0:256] = top
            rs_own[h, 256:512] = low

    def rs_relay(n, h, axis):
        for d in range(2):
            copy(*rs_copy(n, h, 0, d, axis)).wait_recv()
            rs_via_out[n, h, d] = (own_sum[h, 0, d * 256:d * 256 + 256] + rs_far_in[n, h, d].astype(F32)).astype(BF)
            send(*rs_copy(n, h, 2, d, axis))

    def rs_finish(n, h, axis):
        for kind in (1, 2):
            for d in range(2):
                copy(*rs_copy(n, h, kind, d, axis)).wait_recv()
        top = rs_own[h, 0:256] + rs_via_in[n, h, 0].astype(F32) + rs_near_in[n, h, 1].astype(F32)
        low = rs_own[h, 256:512] + rs_near_in[n, h, 0].astype(F32) + rs_via_in[n, h, 1].astype(F32)
        return top, low

    def ag_copy(n, buf, rows, kind, d, axis):
        part = d if kind in (0, 2) else 1 - d
        there = (2, 1)[d]
        here, target = (0, there) if kind < 2 else (there, 3)
        r = pl.ds(part * rows, rows)
        return (buf.at[r, pl.ds(here * 256, 256)], buf.at[r, pl.ds(target * 256, 256)],
                ag_send.at[n, kind, d], ag_recv.at[n, kind, d], axis, d)

    def ag_own(n, buf, rows, axis, part):
        for d in range(2):
            send(*ag_copy(n, buf, rows, 0 if d == part else 1, d, axis))

    def ag_relay(n, buf, rows, axis):
        for d in range(2):
            copy(*ag_copy(n, buf, rows, 0, d, axis)).wait_recv()
            send(*ag_copy(n, buf, rows, 2, d, axis))

    def ag_near(n, buf, rows, axis):
        for d in range(2):
            copy(*ag_copy(n, buf, rows, 1, d, axis)).wait_recv()

    def ag_far(n, buf, rows, axis):
        for d in range(2):
            copy(*ag_copy(n, buf, rows, 2, d, axis)).wait_recv()

    for k, slot in ((0, 3), (1, 1), (2, 2)):
        for h in range(2):
            top, low = first_sum(h, k)
            rs_put(0, h, AXIS2[h], slot, top, low)
    for h in range(2):
        rs_relay(0, h, AXIS2[h])
    for h in range(2):
        top, low = first_sum(h, 3)
        rs_put(0, h, AXIS2[h], 0, top, low)

    squares = jnp.zeros((1, 256), F32)
    for h in range(2):
        top, low = rs_finish(0, h, AXIS2[h])
        grad[h, 0:256] = top
        grad[h, 256:512] = low
        for part, value in ((0, top), (1, low)):
            r = pl.ds(h * 512 + part * 256, 256)
            z_group[r, 0:256] = value.astype(BF)
            y_group[r, 0:256] = value.astype(BF)
            squares += jnp.sum(value * value, axis=0, keepdims=True)
        ag_own(0, z_group, 512, "y", h)
        ag_own(1, y_group, 512, "z", h)

    def sq_copies(n, axis):
        if axis == "core":
            steps = (1,)
        else:
            steps = (1, 2, 3)
        return [
            pltpu.make_async_remote_copy(
                src_ref=sq.at[n, 0], dst_ref=sq.at[n, step],
                send_sem=sq_send.at[n, step], recv_sem=sq_recv.at[n, step],
                device_id=at(axis, step), device_id_type=pl.DeviceIdType.MESH,
            )
            for step in steps
        ]

    def sq_start(n, axis, value):
        sq[n, 0] = jnp.broadcast_to(value, (8, 256))
        for c in sq_copies(n, axis):
            c.start()
            sent.append(c)

    def sq_total(n, axis):
        total = sq[n, 0]
        for step, c in enumerate(sq_copies(n, axis)):
            c.wait_recv()
            total += sq[n, step + 1]
        return total

    sq_start(0, "z", squares)

    ag_relay(0, z_group, 512, "y")
    ag_relay(1, y_group, 512, "z")
    ag_near(0, z_group, 512, "y")
    ag_near(1, y_group, 512, "z")

    def turn(slot):
        a_t[pl.ds(slot * 256, 256), 0:1024] = z_group[:, slot * 256:slot * 256 + 256].T

    for slot in range(3):
        turn(slot)
    sq_start(1, "y", sq_total(0, "z"))
    ag_far(0, z_group, 512, "y")
    ag_far(1, y_group, 512, "z")
    turn(3)

    mine = pl.multiple_of(core * 512, 512)
    other = pl.multiple_of((1 - core) * 512, 512)

    def half_copy(step):
        r = pl.ds(pl.multiple_of(lax.rem(x + step, 4) * 128, 128), 128)
        return half_out.at[r], half_in.at[r], pair_send.at[step], pair_recv.at[step], "core", 0

    def other_body(i, carry):
        cols = pl.ds(pl.multiple_of(i * 256, 256), 256)
        half_out[:, cols] = dot(a_t[pl.ds(other, 512), 0:1024], y_group[:, cols]).astype(BF)
        return carry

    def mine_body(i, carry):
        cols = pl.ds(pl.multiple_of(i * 256, 256), 256)
        tile[:, cols] = dot(a_t[pl.ds(mine, 512), 0:1024], y_group[:, cols])
        return carry

    lax.fori_loop(0, 4, other_body, 0)
    for step in (2, 1, 3, 0):
        send(*half_copy(step))
    lax.fori_loop(0, 4, mine_body, 0)
    sq_start(2, "x", sq_total(1, "y"))

    def pair_sum(step):
        copy(*half_copy(step)).wait_recv()
        r = pl.ds(pl.multiple_of(lax.rem(x + step, 4) * 128, 128), 128)
        return tile[r, :] + half_in[r, :].astype(F32)

    def x_copy(kind, d):
        src, dst = (
            (x_far_out.at[d], x_far_in.at[d]),
            (x_near_out.at[d], x_near_in.at[d]),
            (x_via_out.at[d], x_via_in.at[d]),
        )[kind]
        return src, dst, x_send.at[kind, d], x_recv.at[kind, d], "x", d

    s = pair_sum(2)
    for d in range(2):
        x_far_out[d] = s[:, d * 512:d * 512 + 512].astype(BF)
        send(*x_copy(0, d))
    relayed = []
    for d in range(2):
        s = pair_sum(STEP[d])
        x_near_out[d] = s[:, (1 - d) * 512:(1 - d) * 512 + 512].astype(BF)
        send(*x_copy(1, d))
        r = pl.ds(pl.multiple_of(lax.rem(x + STEP[d], 4) * 128, 128), 128)
        tile[r, d * 512:d * 512 + 512] = s[:, d * 512:d * 512 + 512]
    s = pair_sum(0)
    here = pl.ds(pl.multiple_of(x * 128, 128), 128)
    tile[here, :] = s
    for d in range(2):
        copy(*x_copy(0, d)).wait_recv()
        r = pl.ds(pl.multiple_of(lax.rem(x + STEP[d], 4) * 128, 128), 128)
        x_via_out[d] = (tile[r, d * 512:d * 512 + 512] + x_far_in[d].astype(F32)).astype(BF)
        send(*x_copy(2, d))
    for kind in (1, 2):
        for d in range(2):
            copy(*x_copy(kind, d)).wait_recv()

    def chunk(step, part):
        r = pl.ds(pl.multiple_of(core * 512 + lax.rem(x + step, 4) * 128, 128), 128)
        return gram.at[r, pl.ds(part * 512, 512)]

    chunk(0, 0)[...] = (
        tile[here, 0:512] + x_via_in[0].astype(F32) + x_near_in[1].astype(F32)
    ).astype(BF)
    chunk(0, 1)[...] = (
        tile[here, 512:1024] + x_near_in[0].astype(F32) + x_via_in[1].astype(F32)
    ).astype(BF)

    def gx_copy(kind, d):
        part = d if kind in (0, 2) else 1 - d
        step = 0 if kind < 2 else STEP[1 - d]
        return chunk(step, part), chunk(step, part), gx_send.at[kind, d], gx_recv.at[kind, d], "x", d

    def gx_arrived(kind, d):
        part = d if kind in (0, 2) else 1 - d
        step = STEP[1 - d] if kind < 2 else 2
        ref = chunk(step, part)
        copy(ref, ref, gx_send.at[kind, d], gx_recv.at[kind, d], "x", d).wait_recv()
        return step, part

    def gp_copy(step, part):
        ref = chunk(step, part)
        return ref, ref, gp_send.at[step, part], gp_recv.at[step, part], "core", 0

    for kind in (0, 1):
        for d in range(2):
            send(*gx_copy(kind, d))
    for part in range(2):
        send(*gp_copy(0, part))
    sq_start(3, "core", sq_total(2, "x"))
    arrived = []
    for d in range(2):
        arrived.append(gx_arrived(0, d))
        send(*gx_copy(2, d))
    for d in range(2):
        send(*gp_copy(*arrived[d]))
    for kind in (1, 2):
        for d in range(2):
            send(*gp_copy(*gx_arrived(kind, d)))
    for step in range(4):
        for part in range(2):
            r = pl.ds(pl.multiple_of((1 - core) * 512 + lax.rem(x + step, 4) * 128, 128), 128)
            ref = gram.at[r, pl.ds(part * 512, 512)]
            copy(ref, ref, gp_send.at[step, part], gp_recv.at[step, part], "core", 0).wait_recv()

    total = jnp.sum(sq_total(3, "core")[0:1, :], axis=1, keepdims=True)
    factor = NORM_SHARE * math.sqrt(ROWS) / (jnp.sqrt(total) + NORM_EPSILON)

    def down(lhs, slot):
        return dot(lhs, gram[:, slot * 256:slot * 256 + 256])

    def across(lhs, slot):
        return dot(lhs, gram[slot * 256:slot * 256 + 256, :], NT)

    for slot in (3, 1, 2, 0):
        w = down(z_group[0:512, :], slot)
        rs_put(1, 0, "z", slot, w[0:256], w[256:512])
        w = across(y_group[512:1024, :], slot)
        rs_put(1, 1, "y", slot, w[0:256], w[256:512])
    for h in range(2):
        rs_relay(1, h, AXIS1[h])
    for h in range(2):
        for part, w in enumerate(rs_finish(1, h, AXIS1[h])):
            r = pl.ds(part * 256, 256)
            v = CUBIC_COEF * grad[h, r] + (QUINTIC_COEF * factor * factor) * w
            values[h, r, 0:256] = v.astype(BF)
            ag_own(2 + h, values.at[h], 256, AXIS1[h], part)
    for h in range(2):
        ag_relay(2 + h, values.at[h], 256, AXIS1[h])
    for h in range(2):
        ag_near(2 + h, values.at[h], 256, AXIS1[h])
        ag_far(2 + h, values.at[h], 256, AXIS1[h])
    for slot in (3, 1, 2, 0):
        m = across(values[0], slot)
        rs_put(2, 0, "y", slot, m[0:256], m[256:512])
        m = down(values[1], slot)
        rs_put(2, 1, "z", slot, m[0:256], m[256:512])
    for h in range(2):
        rs_relay(2, h, AXIS2[h])
    scale = math.sqrt(N) * factor
    for h in range(2):
        for part, m in enumerate(rs_finish(2, h, AXIS2[h])):
            r = pl.ds(part * 256, 256)
            o = scale * (LINEAR_COEF * grad[h, r] + (factor * factor) * m)
            out_ref[:, h * 512 + part * 256:h * 512 + part * 256 + 256] = o.T.astype(BF)

    def drain(k, carry):
        for h in range(2):
            for d in range(2):
                far_copy(h, d, k).wait_send()
                near_copy(h, d, k).wait_send()
                via_copy(h, d, k).wait_send()
        return carry

    lax.fori_loop(0, 4, drain, 0)
    for c in sent:
        c.wait_send()


def local(cotangent, activation):
    dma = pltpu.SemaphoreType.DMA
    vm = pltpu.VMEM
    piece = (256, 256)
    return pl.pallas_call(
        kernel,
        out_shape=jax.ShapeDtypeStruct((256, 1024), BF),
        in_specs=[pl.BlockSpec(memory_space=pl.ANY)] * 2,
        out_specs=pl.BlockSpec(memory_space=pltpu.VMEM),
        scratch_shapes=[
            vm((1024, 2048), BF), vm((16, 2048, 256), BF), dma((4,)), dma((16,)),
            vm((2, 4, 512, 256), BF), vm((2, 2, 4) + piece, BF),
            vm((2, 2, 4) + piece, BF), vm((2, 2, 4) + piece, BF),
            vm((2, 2, 4) + piece, BF), vm((2, 2, 4) + piece, BF),
            vm((1024, 1024), F32), vm((2, 4, 512, 256), F32),
            dma((3, 2, 2, 4)), dma((3, 2, 2, 4)),
            vm((3, 2, 512, 256), BF), vm((3, 2, 2) + piece, BF),
            vm((3, 2, 2) + piece, BF), vm((3, 2, 2) + piece, BF),
            vm((3, 2, 2) + piece, BF), vm((3, 2, 2) + piece, BF),
            dma((3, 2, 3, 2)), dma((3, 2, 3, 2)),
            vm((2, 512, 256), F32), vm((1024, 1024), BF), vm((1024, 1024), BF), dma((4, 3, 2)), dma((4, 3, 2)),
            vm((512, 1024), BF), dma((4,)), dma((4,)),
            vm((2, 128, 512), BF), vm((2, 128, 512), BF), vm((2, 128, 512), BF),
            vm((2, 128, 512), BF), vm((2, 128, 512), BF), vm((2, 128, 512), BF), dma((3, 2)), dma((3, 2)),
            vm((1024, 1024), BF), dma((3, 2)), dma((3, 2)), dma((4, 2)), dma((4, 2)),
            vm((2, 512, 1024), BF), vm((4, 4, 8, 256), F32), dma((4, 4)), dma((4, 4)),
        ],
        compiler_params=pltpu.CompilerParams(
            collective_id=0, has_side_effects=True, vmem_limit_bytes=67043328
        ),
        name="muon_step",
    )(cotangent, activation)


def solution(mesh):
    return jax.shard_map(
        local,
        mesh=mesh,
        in_specs=(P("dp", None), P("dp", "mp")),
        out_specs=P("dp", "mp"),
        check_vma=False,
    )
```

```python
import math

import jax
import jax.numpy as jnp
from jax import lax
from jax.experimental import pallas as pl
from jax.experimental.pallas import tpu as pltpu
from jax.sharding import PartitionSpec as P

N = 8192
ROWS = 4096

LINEAR_COEF = 3.4445
CUBIC_COEF = -4.775
QUINTIC_COEF = 2.0315
NORM_EPSILON = 1e-07
NORM_SHARE = 0.25

BF = jnp.bfloat16
F32 = jnp.float32
NN = (((1,), (0,)), ((), ()))
NT = (((1,), (1,)), ((), ()))
FIRST_USE = ((2, 2), (2, 1), (1, 2), (2, 3), (3, 2), (2, 0), (0, 2), (1, 1), (3, 1), (1, 3), (3, 3), (1, 0), (3, 0), (0, 1), (0, 3), (0, 0))
LATE = FIRST_USE[12:]
PLUS, MINUS = 0, 1


def dot(a, b, dims=NN):
    return lax.dot_general(a, b, dims, preferred_element_type=F32)


def kernel(
    c_ref, a_ref, out_ref,
    a_t, c_in, a_sem, c_sem,
    far_out, far_in, near_out, near_in, via_out, via_in, via_sum, own_sum, g_send, g_recv,
    rs_far_out, rs_far_in, rs_near_out, rs_near_in, rs_via_out, rs_via_in, rs_send, rs_recv,
    grad, z_group, y_group, ag_send, ag_recv,
    half_in, pair_send, pair_recv,
    x_far_out, x_far_in, x_near_out, x_near_in, x_via_out, x_via_in, x_send, x_recv,
    gram, gx_send, gx_recv, gp_send, gp_recv,
    values, sq, sq_send, sq_recv,
):
    dp, mp = lax.axis_index("dp"), lax.axis_index("mp")
    z, y = dp // 4, lax.rem(dp, 4)
    x, core = mp // 2, lax.rem(mp, 2)

    def at(axis, step):
        if axis == "z":
            return (lax.rem(z + step, 4) * 4 + y, mp)
        if axis == "y":
            return (z * 4 + lax.rem(y + step, 4), mp)
        if axis == "x":
            return (dp, lax.rem(x + step, 4) * 2 + core)
        return (dp, x * 2 + 1 - core)

    STEP = (1, 3)
    sent = []

    def copy(src, dst, send, recv, axis, direction):
        return pltpu.make_async_remote_copy(
            src_ref=src, dst_ref=dst, send_sem=send, recv_sem=recv,
            device_id=at(axis, STEP[direction]), device_id_type=pl.DeviceIdType.MESH,
        )

    def send(*args):
        c = copy(*args)
        c.start()
        sent.append(c)
        return c

    tile = via_sum.at[0:512]
    half_out = a_t.at[0:512, 1024:2048]
    rs_own = own_sum.at[:, 1]

    def load_a(q):
        slot = 4 * LATE[q][0] + LATE[q][1]
        return pltpu.make_async_copy(a_ref.at[:, pl.ds(q * 256, 256)], c_in.at[slot], a_sem.at[q])

    def pick(k):
        return jnp.where(k == 0, 2, jnp.where(k == 1, 1, jnp.where(k == 2, 3, 0)))

    def load_c(dz, dy):
        slot = 4 * dz + dy
        col = pl.multiple_of((4 * lax.rem(z + dz, 4) + lax.rem(y + dy, 4)) * 256, 256)
        return pltpu.make_async_copy(c_ref.at[:, pl.ds(col, 256)], c_in.at[slot], c_sem.at[slot])

    for q in range(4):
        load_a(q).start()
    for dz, dy in FIRST_USE[:12]:
        load_c(dz, dy).start()

    barrier = pltpu.get_barrier_semaphore()
    for axis in ("z", "y", "x"):
        for step in (1, 2, 3):
            pl.semaphore_signal(barrier, inc=1, device_id=at(axis, step), device_id_type=pl.DeviceIdType.MESH)
    pl.semaphore_signal(barrier, inc=1, device_id=at("core", 0), device_id_type=pl.DeviceIdType.MESH)

    for q in range(4):
        load_a(q).wait()
        a_t[pl.ds(q * 256, 256), :] = c_in[4 * LATE[q][0] + LATE[q][1]].T
        load_c(*LATE[q]).start()
    pl.semaphore_wait(barrier, 10)

    AXIS1 = ("z", "y")
    AXIS2 = ("y", "z")

    def unit(h, step, k):
        slot = 4 * step + pick(k) if h == 0 else 4 * pick(k) + step
        return dot(a_t[pl.ds(h * 512, 512), :], c_in[slot])

    def far_copy(h, d, k):
        return copy(far_out.at[h, k, pl.ds(d * 256, 256)], far_in.at[h, d, k],
                    g_send.at[0, h, d, k], g_recv.at[0, h, d, k], AXIS1[h], d)

    def near_copy(h, d, k):
        return copy(near_out.at[h, d, k], near_in.at[h, d, k],
                    g_send.at[1, h, d, k], g_recv.at[1, h, d, k], AXIS1[h], d)

    def via_copy(h, d, k):
        return copy(via_out.at[h, d, k], via_in.at[h, d, k],
                    g_send.at[2, h, d, k], g_recv.at[2, h, d, k], AXIS1[h], d)

    def far_body(k, carry):
        load_c(2, pick(k)).wait()

        @pl.when(k > 0)
        def _():
            load_c(pick(k), 2).wait()

        for h in range(2):
            far_out[h, k] = unit(h, 2, k).astype(BF)
            for d in range(2):
                far_copy(h, d, k).start()
        return carry

    def piece(h, d, k):
        return pl.ds((2 * h + d) * 256, 256), pl.ds(pl.multiple_of(k * 256, 256), 256)

    def via_body(k, carry):
        for h in range(2):
            for d in range(2):
                far_copy(h, d, k).wait_recv()
                via_out[h, d, k] = (via_sum[piece(h, d, k)] + far_in[h, d, k].astype(F32)).astype(BF)
                via_copy(h, d, k).start()
        return carry

    def near_body(k, carry):
        for when, blocks in ((1, FIRST_USE[7:10]), (2, FIRST_USE[10:11]), (3, FIRST_USE[11:15])):
            @pl.when(k == when)
            def _():
                for dz, dy in blocks:
                    load_c(dz, dy).wait()

        for h in range(2):
            for d in range(2):
                r = unit(h, 1 + 2 * d, k)
                direct, relayed = 1 - d, d
                near_out[h, d, k] = r[direct * 256:direct * 256 + 256].astype(BF)
                via_sum[piece(h, d, k)] = r[relayed * 256:relayed * 256 + 256]
                near_copy(h, d, k).start()
        return via_body(k, carry)

    def own_body(k, carry):
        @pl.when(k == 3)
        def _():
            load_c(0, 0).wait()

        for h in range(2):
            own_sum[h, k] = unit(h, 0, k)
        return carry

    lax.fori_loop(0, 4, far_body, 0)
    lax.fori_loop(0, 4, near_body, 0)
    lax.fori_loop(0, 4, own_body, 0)

    def first_sum(h, k):
        for d in range(2):
            near_copy(h, d, k).wait_recv()
            via_copy(h, d, k).wait_recv()
        top = own_sum[h, k, 0:256] + via_in[h, 0, k].astype(F32) + near_in[h, 1, k].astype(F32)
        low = own_sum[h, k, 256:512] + near_in[h, 0, k].astype(F32) + via_in[h, 1, k].astype(F32)
        return top, low

    def rs_copy(n, h, kind, d, axis):
        src, dst = (
            (rs_far_out.at[n, h, pl.ds(d * 256, 256)], rs_far_in.at[n, h, d]),
            (rs_near_out.at[n, h, d], rs_near_in.at[n, h, d]),
            (rs_via_out.at[n, h, d], rs_via_in.at[n, h, d]),
        )[kind]
        return src, dst, rs_send.at[n, h, kind, d], rs_recv.at[n, h, kind, d], axis, d

    def rs_put(n, h, axis, slot, top, low):
        if slot == 3:
            rs_far_out[n, h, 0:256] = top.astype(BF)
            rs_far_out[n, h, 256:512] = low.astype(BF)
            for d in range(2):
                send(*rs_copy(n, h, 0, d, axis))
        elif slot == 1:
            rs_near_out[n, h, 0] = low.astype(BF)
            send(*rs_copy(n, h, 1, 0, axis))
            own_sum[h, 0, 0:256] = top
        elif slot == 2:
            rs_near_out[n, h, 1] = top.astype(BF)
            send(*rs_copy(n, h, 1, 1, axis))
            own_sum[h, 0, 256:512] = low
        else:
            rs_own[h, 0:256] = top
            rs_own[h, 256:512] = low

    def rs_relay(n, h, axis):
        for d in range(2):
            copy(*rs_copy(n, h, 0, d, axis)).wait_recv()
            rs_via_out[n, h, d] = (own_sum[h, 0, d * 256:d * 256 + 256] + rs_far_in[n, h, d].astype(F32)).astype(BF)
            send(*rs_copy(n, h, 2, d, axis))

    def rs_finish(n, h, axis):
        for kind in (1, 2):
            for d in range(2):
                copy(*rs_copy(n, h, kind, d, axis)).wait_recv()
        top = rs_own[h, 0:256] + rs_via_in[n, h, 0].astype(F32) + rs_near_in[n, h, 1].astype(F32)
        low = rs_own[h, 256:512] + rs_near_in[n, h, 0].astype(F32) + rs_via_in[n, h, 1].astype(F32)
        return top, low

    def ag_copy(n, buf, rows, kind, d, axis):
        part = d if kind in (0, 2) else 1 - d
        there = (2, 1)[d]
        here, target = (0, there) if kind < 2 else (there, 3)
        r = pl.ds(part * rows, rows)
        return (buf.at[r, pl.ds(here * 256, 256)], buf.at[r, pl.ds(target * 256, 256)],
                ag_send.at[n, kind, d], ag_recv.at[n, kind, d], axis, d)

    def ag_own(n, buf, rows, axis, part):
        for d in range(2):
            send(*ag_copy(n, buf, rows, 0 if d == part else 1, d, axis))

    def ag_relay(n, buf, rows, axis):
        for d in range(2):
            copy(*ag_copy(n, buf, rows, 0, d, axis)).wait_recv()
            send(*ag_copy(n, buf, rows, 2, d, axis))

    def ag_near(n, buf, rows, axis):
        for d in range(2):
            copy(*ag_copy(n, buf, rows, 1, d, axis)).wait_recv()

    def ag_far(n, buf, rows, axis):
        for d in range(2):
            copy(*ag_copy(n, buf, rows, 2, d, axis)).wait_recv()

    for k, slot in ((0, 3), (1, 1), (2, 2)):
        for h in range(2):
            top, low = first_sum(h, k)
            rs_put(0, h, AXIS2[h], slot, top, low)
    for h in range(2):
        rs_relay(0, h, AXIS2[h])
    for h in range(2):
        top, low = first_sum(h, 3)
        rs_put(0, h, AXIS2[h], 0, top, low)

    squares = jnp.zeros((1, 256), F32)
    for h in range(2):
        top, low = rs_finish(0, h, AXIS2[h])
        grad[h, 0:256] = top
        grad[h, 256:512] = low
        for part, value in ((0, top), (1, low)):
            r = pl.ds(h * 512 + part * 256, 256)
            z_group[r, 0:256] = value.astype(BF)
            y_group[r, 0:256] = value.astype(BF)
            squares += jnp.sum(value * value, axis=0, keepdims=True)
        ag_own(0, z_group, 512, "y", h)
        ag_own(1, y_group, 512, "z", h)

    def sq_copies(n, axis):
        if axis == "core":
            steps = (1,)
        else:
            steps = (1, 2, 3)
        return [
            pltpu.make_async_remote_copy(
                src_ref=sq.at[n, 0], dst_ref=sq.at[n, step],
                send_sem=sq_send.at[n, step], recv_sem=sq_recv.at[n, step],
                device_id=at(axis, step), device_id_type=pl.DeviceIdType.MESH,
            )
            for step in steps
        ]

    def sq_start(n, axis, value):
        sq[n, 0] = jnp.broadcast_to(value, (8, 256))
        for c in sq_copies(n, axis):
            c.start()
            sent.append(c)

    def sq_total(n, axis):
        total = sq[n, 0]
        for step, c in enumerate(sq_copies(n, axis)):
            c.wait_recv()
            total += sq[n, step + 1]
        return total

    sq_start(0, "z", squares)

    ag_relay(0, z_group, 512, "y")
    ag_relay(1, y_group, 512, "z")
    ag_near(0, z_group, 512, "y")
    ag_near(1, y_group, 512, "z")

    def turn(slot):
        a_t[pl.ds(slot * 256, 256), 0:1024] = z_group[:, slot * 256:slot * 256 + 256].T

    for slot in range(3):
        turn(slot)
    sq_start(1, "y", sq_total(0, "z"))
    ag_far(0, z_group, 512, "y")
    ag_far(1, y_group, 512, "z")
    turn(3)

    mine = pl.multiple_of(core * 512, 512)
    other = pl.multiple_of((1 - core) * 512, 512)

    def half_copy(step):
        r = pl.ds(pl.multiple_of(lax.rem(x + step, 4) * 128, 128), 128)
        return half_out.at[r], half_in.at[r], pair_send.at[step], pair_recv.at[step], "core", 0

    def other_body(i, carry):
        cols = pl.ds(pl.multiple_of(i * 256, 256), 256)
        half_out[:, cols] = dot(a_t[pl.ds(other, 512), 0:1024], y_group[:, cols]).astype(BF)
        return carry

    def mine_body(i, carry):
        cols = pl.ds(pl.multiple_of(i * 256, 256), 256)
        tile[:, cols] = dot(a_t[pl.ds(mine, 512), 0:1024], y_group[:, cols])
        return carry

    lax.fori_loop(0, 4, other_body, 0)
    for step in (2, 1, 3, 0):
        send(*half_copy(step))
    lax.fori_loop(0, 4, mine_body, 0)
    sq_start(2, "x", sq_total(1, "y"))

    def pair_sum(step):
        copy(*half_copy(step)).wait_recv()
        r = pl.ds(pl.multiple_of(lax.rem(x + step, 4) * 128, 128), 128)
        return tile[r, :] + half_in[r, :].astype(F32)

    def x_copy(kind, d):
        src, dst = (
            (x_far_out.at[d], x_far_in.at[d]),
            (x_near_out.at[d], x_near_in.at[d]),
            (x_via_out.at[d], x_via_in.at[d]),
        )[kind]
        return src, dst, x_send.at[kind, d], x_recv.at[kind, d], "x", d

    s = pair_sum(2)
    for d in range(2):
        x_far_out[d] = s[:, d * 512:d * 512 + 512].astype(BF)
        send(*x_copy(0, d))
    relayed = []
    for d in range(2):
        s = pair_sum(STEP[d])
        x_near_out[d] = s[:, (1 - d) * 512:(1 - d) * 512 + 512].astype(BF)
        send(*x_copy(1, d))
        r = pl.ds(pl.multiple_of(lax.rem(x + STEP[d], 4) * 128, 128), 128)
        tile[r, d * 512:d * 512 + 512] = s[:, d * 512:d * 512 + 512]
    s = pair_sum(0)
    here = pl.ds(pl.multiple_of(x * 128, 128), 128)
    tile[here, :] = s
    for d in range(2):
        copy(*x_copy(0, d)).wait_recv()
        r = pl.ds(pl.multiple_of(lax.rem(x + STEP[d], 4) * 128, 128), 128)
        x_via_out[d] = (tile[r, d * 512:d * 512 + 512] + x_far_in[d].astype(F32)).astype(BF)
        send(*x_copy(2, d))
    for kind in (1, 2):
        for d in range(2):
            copy(*x_copy(kind, d)).wait_recv()

    def chunk(step, part):
        r = pl.ds(pl.multiple_of(core * 512 + lax.rem(x + step, 4) * 128, 128), 128)
        return gram.at[r, pl.ds(part * 512, 512)]

    chunk(0, 0)[...] = (
        tile[here, 0:512] + x_via_in[0].astype(F32) + x_near_in[1].astype(F32)
    ).astype(BF)
    chunk(0, 1)[...] = (
        tile[here, 512:1024] + x_near_in[0].astype(F32) + x_via_in[1].astype(F32)
    ).astype(BF)

    def gx_copy(kind, d):
        part = d if kind in (0, 2) else 1 - d
        step = 0 if kind < 2 else STEP[1 - d]
        return chunk(step, part), chunk(step, part), gx_send.at[kind, d], gx_recv.at[kind, d], "x", d

    def gx_arrived(kind, d):
        part = d if kind in (0, 2) else 1 - d
        step = STEP[1 - d] if kind < 2 else 2
        ref = chunk(step, part)
        copy(ref, ref, gx_send.at[kind, d], gx_recv.at[kind, d], "x", d).wait_recv()
        return step, part

    def gp_copy(step, part):
        ref = chunk(step, part)
        return ref, ref, gp_send.at[step, part], gp_recv.at[step, part], "core", 0

    for kind in (0, 1):
        for d in range(2):
            send(*gx_copy(kind, d))
    for part in range(2):
        send(*gp_copy(0, part))
    sq_start(3, "core", sq_total(2, "x"))
    arrived = []
    for d in range(2):
        arrived.append(gx_arrived(0, d))
        send(*gx_copy(2, d))
    for d in range(2):
        send(*gp_copy(*arrived[d]))
    for kind in (1, 2):
        for d in range(2):
            send(*gp_copy(*gx_arrived(kind, d)))
    for step in range(4):
        for part in range(2):
            r = pl.ds(pl.multiple_of((1 - core) * 512 + lax.rem(x + step, 4) * 128, 128), 128)
            ref = gram.at[r, pl.ds(part * 512, 512)]
            copy(ref, ref, gp_send.at[step, part], gp_recv.at[step, part], "core", 0).wait_recv()

    total = jnp.sum(sq_total(3, "core")[0:1, :], axis=1, keepdims=True)
    factor = NORM_SHARE * math.sqrt(ROWS) / (jnp.sqrt(total) + NORM_EPSILON)

    def down(lhs, slot):
        return dot(lhs, gram[:, slot * 256:slot * 256 + 256])

    def across(lhs, slot):
        return dot(lhs, gram[slot * 256:slot * 256 + 256, :], NT)

    for slot in (3, 1, 2, 0):
        w = down(z_group[0:512, :], slot)
        rs_put(1, 0, "z", slot, w[0:256], w[256:512])
        w = across(y_group[512:1024, :], slot)
        rs_put(1, 1, "y", slot, w[0:256], w[256:512])
    for h in range(2):
        rs_relay(1, h, AXIS1[h])
    for h in range(2):
        for part, w in enumerate(rs_finish(1, h, AXIS1[h])):
            r = pl.ds(part * 256, 256)
            v = CUBIC_COEF * grad[h, r] + (QUINTIC_COEF * factor * factor) * w
            values[h, r, 0:256] = v.astype(BF)
            ag_own(2 + h, values.at[h], 256, AXIS1[h], part)
    for h in range(2):
        ag_relay(2 + h, values.at[h], 256, AXIS1[h])
    for h in range(2):
        ag_near(2 + h, values.at[h], 256, AXIS1[h])
        ag_far(2 + h, values.at[h], 256, AXIS1[h])
    for slot in (3, 1, 2, 0):
        m = across(values[0], slot)
        rs_put(2, 0, "y", slot, m[0:256], m[256:512])
        m = down(values[1], slot)
        rs_put(2, 1, "z", slot, m[0:256], m[256:512])
    for h in range(2):
        rs_relay(2, h, AXIS2[h])
    scale = math.sqrt(N) * factor
    for h in range(2):
        for part, m in enumerate(rs_finish(2, h, AXIS2[h])):
            r = pl.ds(part * 256, 256)
            o = scale * (LINEAR_COEF * grad[h, r] + (factor * factor) * m)
            out_ref[:, h * 512 + part * 256:h * 512 + part * 256 + 256] = o.T.astype(BF)

    def drain(k, carry):
        for h in range(2):
            for d in range(2):
                far_copy(h, d, k).wait_send()
                near_copy(h, d, k).wait_send()
                via_copy(h, d, k).wait_send()
        return carry

    lax.fori_loop(0, 4, drain, 0)
    for c in sent:
        c.wait_send()


def local(cotangent, activation):
    dma = pltpu.SemaphoreType.DMA
    vm = pltpu.VMEM
    piece = (256, 256)
    return pl.pallas_call(
        kernel,
        out_shape=jax.ShapeDtypeStruct((256, 1024), BF),
        in_specs=[pl.BlockSpec(memory_space=pl.ANY)] * 2,
        out_specs=pl.BlockSpec(memory_space=pltpu.VMEM),
        scratch_shapes=[
            vm((1024, 2048), BF), vm((16, 2048, 256), BF), dma((4,)), dma((16,)),
            vm((2, 4, 512, 256), BF), vm((2, 2, 4) + piece, BF),
            vm((2, 2, 4) + piece, BF), vm((2, 2, 4) + piece, BF),
            vm((2, 2, 4) + piece, BF), vm((2, 2, 4) + piece, BF),
            vm((1024, 1024), F32), vm((2, 4, 512, 256), F32),
            dma((3, 2, 2, 4)), dma((3, 2, 2, 4)),
            vm((3, 2, 512, 256), BF), vm((3, 2, 2) + piece, BF),
            vm((3, 2, 2) + piece, BF), vm((3, 2, 2) + piece, BF),
            vm((3, 2, 2) + piece, BF), vm((3, 2, 2) + piece, BF),
            dma((3, 2, 3, 2)), dma((3, 2, 3, 2)),
            vm((2, 512, 256), F32), vm((1024, 1024), BF), vm((1024, 1024), BF), dma((4, 3, 2)), dma((4, 3, 2)),
            vm((512, 1024), BF), dma((4,)), dma((4,)),
            vm((2, 128, 512), BF), vm((2, 128, 512), BF), vm((2, 128, 512), BF),
            vm((2, 128, 512), BF), vm((2, 128, 512), BF), vm((2, 128, 512), BF), dma((3, 2)), dma((3, 2)),
            vm((1024, 1024), BF), dma((3, 2)), dma((3, 2)), dma((4, 2)), dma((4, 2)),
            vm((2, 512, 1024), BF), vm((4, 4, 8, 256), F32), dma((4, 4)), dma((4, 4)),
        ],
        compiler_params=pltpu.CompilerParams(
            collective_id=0, has_side_effects=True, vmem_limit_bytes=67043328
        ),
        name="muon_step",
    )(cotangent, activation)


def solution(mesh):
    return jax.shard_map(
        local,
        mesh=mesh,
        in_specs=(P("dp", None), P("dp", "mp")),
        out_specs=P("dp", "mp"),
        check_vma=False,
    )
```

```python
import math

import jax
import jax.numpy as jnp
from jax import lax
from jax.experimental import pallas as pl
from jax.experimental.pallas import tpu as pltpu
from jax.sharding import PartitionSpec as P

N = 8192
ROWS = 4096

LINEAR_COEF = 3.4445
CUBIC_COEF = -4.775
QUINTIC_COEF = 2.0315
NORM_EPSILON = 1e-07
NORM_SHARE = 0.25

BF = jnp.bfloat16
F32 = jnp.float32
NN = (((1,), (0,)), ((), ()))
NT = (((1,), (1,)), ((), ()))
FIRST_USE = ((2, 2), (2, 1), (1, 2), (2, 3), (3, 2), (2, 0), (0, 2), (1, 1), (3, 1), (1, 3), (3, 3), (1, 0), (3, 0), (0, 1), (0, 3), (0, 0))
LATE = FIRST_USE[12:]
PLUS, MINUS = 0, 1


def dot(a, b, dims=NN):
    return lax.dot_general(a, b, dims, preferred_element_type=F32)


def kernel(
    c_ref, a_ref, out_ref,
    a_t, c_in, a_sem, c_sem,
    far_out, far_in, near_out, near_in, via_out, via_in, via_sum, own_sum, g_send, g_recv,
    rs_far_out, rs_far_in, rs_near_out, rs_near_in, rs_via_out, rs_via_in, rs_send, rs_recv,
    grad, z_group, y_group, ag_send, ag_recv,
    half_in, pair_send, pair_recv,
    x_far_out, x_far_in, x_near_out, x_near_in, x_via_out, x_via_in, x_send, x_recv,
    gram, gx_send, gx_recv, gp_send, gp_recv,
    values, sq, sq_send, sq_recv,
):
    dp, mp = lax.axis_index("dp"), lax.axis_index("mp")
    z, y = dp // 4, lax.rem(dp, 4)
    x, core = mp // 2, lax.rem(mp, 2)

    def at(axis, step):
        if axis == "z":
            return (lax.rem(z + step, 4) * 4 + y, mp)
        if axis == "y":
            return (z * 4 + lax.rem(y + step, 4), mp)
        if axis == "x":
            return (dp, lax.rem(x + step, 4) * 2 + core)
        return (dp, x * 2 + 1 - core)

    STEP = (1, 3)
    sent = []

    def copy(src, dst, send, recv, axis, direction):
        return pltpu.make_async_remote_copy(
            src_ref=src, dst_ref=dst, send_sem=send, recv_sem=recv,
            device_id=at(axis, STEP[direction]), device_id_type=pl.DeviceIdType.MESH,
        )

    def send(*args):
        c = copy(*args)
        c.start()
        sent.append(c)
        return c

    tile = via_sum.at[0:512]
    half_out = a_t.at[0:512, 1024:2048]
    rs_own = own_sum.at[:, 1]

    def load_a(q):
        slot = 4 * LATE[q][0] + LATE[q][1]
        return pltpu.make_async_copy(a_ref.at[:, pl.ds(q * 256, 256)], c_in.at[slot], a_sem.at[q])

    def pick(k):
        return jnp.where(k == 0, 2, jnp.where(k == 1, 1, jnp.where(k == 2, 3, 0)))

    def load_c(dz, dy):
        slot = 4 * dz + dy
        col = pl.multiple_of((4 * lax.rem(z + dz, 4) + lax.rem(y + dy, 4)) * 256, 256)
        return pltpu.make_async_copy(c_ref.at[:, pl.ds(col, 256)], c_in.at[slot], c_sem.at[slot])

    for q in range(4):
        load_a(q).start()
    for dz, dy in FIRST_USE[:12]:
        load_c(dz, dy).start()

    barrier = pltpu.get_barrier_semaphore()
    for axis in ("z", "y", "x"):
        for step in (1, 2, 3):
            pl.semaphore_signal(barrier, inc=1, device_id=at(axis, step), device_id_type=pl.DeviceIdType.MESH)
    pl.semaphore_signal(barrier, inc=1, device_id=at("core", 0), device_id_type=pl.DeviceIdType.MESH)

    for q in range(4):
        load_a(q).wait()
        a_t[pl.ds(q * 256, 256), :] = c_in[4 * LATE[q][0] + LATE[q][1]].T
        load_c(*LATE[q]).start()
    pl.semaphore_wait(barrier, 10)

    AXIS1 = ("z", "y")
    AXIS2 = ("y", "z")

    def unit(h, step, k):
        slot = 4 * step + pick(k) if h == 0 else 4 * pick(k) + step
        return dot(a_t[pl.ds(h * 512, 512), :], c_in[slot])

    def far_copy(h, d, k):
        return copy(far_out.at[h, k, pl.ds(d * 256, 256)], far_in.at[h, d, k],
                    g_send.at[0, h, d, k], g_recv.at[0, h, d, k], AXIS1[h], d)

    def near_copy(h, d, k):
        return copy(near_out.at[h, d, k], near_in.at[h, d, k],
                    g_send.at[1, h, d, k], g_recv.at[1, h, d, k], AXIS1[h], d)

    def via_copy(h, d, k):
        return copy(via_out.at[h, d, k], via_in.at[h, d, k],
                    g_send.at[2, h, d, k], g_recv.at[2, h, d, k], AXIS1[h], d)

    def far_body(k, carry):
        load_c(2, pick(k)).wait()

        @pl.when(k > 0)
        def _():
            load_c(pick(k), 2).wait()

        for h in range(2):
            far_out[h, k] = unit(h, 2, k).astype(BF)
            for d in range(2):
                far_copy(h, d, k).start()
        return carry

    def piece(h, d, k):
        return pl.ds((2 * h + d) * 256, 256), pl.ds(pl.multiple_of(k * 256, 256), 256)

    def via_body(k, carry):
        for h in range(2):
            for d in range(2):
                far_copy(h, d, k).wait_recv()
                via_out[h, d, k] = (via_sum[piece(h, d, k)] + far_in[h, d, k].astype(F32)).astype(BF)
                via_copy(h, d, k).start()
        return carry

    def near_body(k, carry):
        for when, blocks in ((1, FIRST_USE[7:10]), (2, FIRST_USE[10:11]), (3, FIRST_USE[11:15])):
            @pl.when(k == when)
            def _():
                for dz, dy in blocks:
                    load_c(dz, dy).wait()

        for h in range(2):
            for d in range(2):
                r = unit(h, 1 + 2 * d, k)
                direct, relayed = 1 - d, d
                near_out[h, d, k] = r[direct * 256:direct * 256 + 256].astype(BF)
                via_sum[piece(h, d, k)] = r[relayed * 256:relayed * 256 + 256]
                near_copy(h, d, k).start()
        return via_body(k, carry)

    def own_body(k, carry):
        @pl.when(k == 3)
        def _():
            load_c(0, 0).wait()

        for h in range(2):
            own_sum[h, k] = unit(h, 0, k)
        return carry

    lax.fori_loop(0, 4, far_body, 0)
    lax.fori_loop(0, 4, near_body, 0)

    def first_sum(h, k):
        for d in range(2):
            near_copy(h, d, k).wait_recv()
            via_copy(h, d, k).wait_recv()
        top = own_sum[h, k, 0:256] + via_in[h, 0, k].astype(F32) + near_in[h, 1, k].astype(F32)
        low = own_sum[h, k, 256:512] + near_in[h, 0, k].astype(F32) + via_in[h, 1, k].astype(F32)
        return top, low

    def rs_copy(n, h, kind, d, axis):
        src, dst = (
            (rs_far_out.at[n, h, pl.ds(d * 256, 256)], rs_far_in.at[n, h, d]),
            (rs_near_out.at[n, h, d], rs_near_in.at[n, h, d]),
            (rs_via_out.at[n, h, d], rs_via_in.at[n, h, d]),
        )[kind]
        return src, dst, rs_send.at[n, h, kind, d], rs_recv.at[n, h, kind, d], axis, d

    def rs_put(n, h, axis, slot, top, low):
        if slot == 3:
            rs_far_out[n, h, 0:256] = top.astype(BF)
            rs_far_out[n, h, 256:512] = low.astype(BF)
            for d in range(2):
                send(*rs_copy(n, h, 0, d, axis))
        elif slot == 1:
            rs_near_out[n, h, 0] = low.astype(BF)
            send(*rs_copy(n, h, 1, 0, axis))
            own_sum[h, 0, 0:256] = top
        elif slot == 2:
            rs_near_out[n, h, 1] = top.astype(BF)
            send(*rs_copy(n, h, 1, 1, axis))
            own_sum[h, 0, 256:512] = low
        else:
            rs_own[h, 0:256] = top
            rs_own[h, 256:512] = low

    def rs_relay(n, h, axis):
        for d in range(2):
            copy(*rs_copy(n, h, 0, d, axis)).wait_recv()
            rs_via_out[n, h, d] = (own_sum[h, 0, d * 256:d * 256 + 256] + rs_far_in[n, h, d].astype(F32)).astype(BF)
            send(*rs_copy(n, h, 2, d, axis))

    def rs_finish(n, h, axis):
        for kind in (1, 2):
            for d in range(2):
                copy(*rs_copy(n, h, kind, d, axis)).wait_recv()
        top = rs_own[h, 0:256] + rs_via_in[n, h, 0].astype(F32) + rs_near_in[n, h, 1].astype(F32)
        low = rs_own[h, 256:512] + rs_near_in[n, h, 0].astype(F32) + rs_via_in[n, h, 1].astype(F32)
        return top, low

    def ag_copy(n, buf, rows, kind, d, axis):
        part = d if kind in (0, 2) else 1 - d
        there = (2, 1)[d]
        here, target = (0, there) if kind < 2 else (there, 3)
        r = pl.ds(part * rows, rows)
        return (buf.at[r, pl.ds(here * 256, 256)], buf.at[r, pl.ds(target * 256, 256)],
                ag_send.at[n, kind, d], ag_recv.at[n, kind, d], axis, d)

    def ag_own(n, buf, rows, axis, part):
        for d in range(2):
            send(*ag_copy(n, buf, rows, 0 if d == part else 1, d, axis))

    def ag_relay(n, buf, rows, axis):
        for d in range(2):
            copy(*ag_copy(n, buf, rows, 0, d, axis)).wait_recv()
            send(*ag_copy(n, buf, rows, 2, d, axis))

    def ag_near(n, buf, rows, axis):
        for d in range(2):
            copy(*ag_copy(n, buf, rows, 1, d, axis)).wait_recv()

    def ag_far(n, buf, rows, axis):
        for d in range(2):
            copy(*ag_copy(n, buf, rows, 2, d, axis)).wait_recv()

    for k, slot in ((0, 3), (1, 1), (2, 2)):
        own_body(jnp.int32(k), 0)
        for h in range(2):
            top, low = first_sum(h, k)
            rs_put(0, h, AXIS2[h], slot, top, low)
    own_body(jnp.int32(3), 0)
    for h in range(2):
        rs_relay(0, h, AXIS2[h])
    for h in range(2):
        top, low = first_sum(h, 3)
        rs_put(0, h, AXIS2[h], 0, top, low)

    squares = jnp.zeros((1, 256), F32)
    for h in range(2):
        top, low = rs_finish(0, h, AXIS2[h])
        grad[h, 0:256] = top
        grad[h, 256:512] = low
        for part, value in ((0, top), (1, low)):
            r = pl.ds(h * 512 + part * 256, 256)
            z_group[r, 0:256] = value.astype(BF)
            y_group[r, 0:256] = value.astype(BF)
            squares += jnp.sum(value * value, axis=0, keepdims=True)
        ag_own(0, z_group, 512, "y", h)
        ag_own(1, y_group, 512, "z", h)

    def sq_copies(n, axis):
        if axis == "core":
            steps = (1,)
        else:
            steps = (1, 2, 3)
        return [
            pltpu.make_async_remote_copy(
                src_ref=sq.at[n, 0], dst_ref=sq.at[n, step],
                send_sem=sq_send.at[n, step], recv_sem=sq_recv.at[n, step],
                device_id=at(axis, step), device_id_type=pl.DeviceIdType.MESH,
            )
            for step in steps
        ]

    def sq_start(n, axis, value):
        sq[n, 0] = jnp.broadcast_to(value, (8, 256))
        for c in sq_copies(n, axis):
            c.start()
            sent.append(c)

    def sq_total(n, axis):
        total = sq[n, 0]
        for step, c in enumerate(sq_copies(n, axis)):
            c.wait_recv()
            total += sq[n, step + 1]
        return total

    sq_start(0, "z", squares)

    ag_relay(0, z_group, 512, "y")
    ag_relay(1, y_group, 512, "z")
    ag_near(0, z_group, 512, "y")
    ag_near(1, y_group, 512, "z")

    def turn(slot):
        a_t[pl.ds(slot * 256, 256), 0:1024] = z_group[:, slot * 256:slot * 256 + 256].T

    for slot in range(3):
        turn(slot)
    sq_start(1, "y", sq_total(0, "z"))
    ag_far(0, z_group, 512, "y")
    ag_far(1, y_group, 512, "z")
    turn(3)

    mine = pl.multiple_of(core * 512, 512)
    other = pl.multiple_of((1 - core) * 512, 512)

    def half_copy(step):
        r = pl.ds(pl.multiple_of(lax.rem(x + step, 4) * 128, 128), 128)
        return half_out.at[r], half_in.at[r], pair_send.at[step], pair_recv.at[step], "core", 0

    def other_body(i, carry):
        cols = pl.ds(pl.multiple_of(i * 256, 256), 256)
        half_out[:, cols] = dot(a_t[pl.ds(other, 512), 0:1024], y_group[:, cols]).astype(BF)
        return carry

    def mine_body(i, carry):
        cols = pl.ds(pl.multiple_of(i * 256, 256), 256)
        tile[:, cols] = dot(a_t[pl.ds(mine, 512), 0:1024], y_group[:, cols])
        return carry

    lax.fori_loop(0, 4, other_body, 0)
    for step in (2, 1, 3, 0):
        send(*half_copy(step))
    lax.fori_loop(0, 4, mine_body, 0)
    sq_start(2, "x", sq_total(1, "y"))

    def pair_sum(step):
        copy(*half_copy(step)).wait_recv()
        r = pl.ds(pl.multiple_of(lax.rem(x + step, 4) * 128, 128), 128)
        return tile[r, :] + half_in[r, :].astype(F32)

    def x_copy(kind, d):
        src, dst = (
            (x_far_out.at[d], x_far_in.at[d]),
            (x_near_out.at[d], x_near_in.at[d]),
            (x_via_out.at[d], x_via_in.at[d]),
        )[kind]
        return src, dst, x_send.at[kind, d], x_recv.at[kind, d], "x", d

    s = pair_sum(2)
    for d in range(2):
        x_far_out[d] = s[:, d * 512:d * 512 + 512].astype(BF)
        send(*x_copy(0, d))
    relayed = []
    for d in range(2):
        s = pair_sum(STEP[d])
        x_near_out[d] = s[:, (1 - d) * 512:(1 - d) * 512 + 512].astype(BF)
        send(*x_copy(1, d))
        r = pl.ds(pl.multiple_of(lax.rem(x + STEP[d], 4) * 128, 128), 128)
        tile[r, d * 512:d * 512 + 512] = s[:, d * 512:d * 512 + 512]
    s = pair_sum(0)
    here = pl.ds(pl.multiple_of(x * 128, 128), 128)
    tile[here, :] = s
    for d in range(2):
        copy(*x_copy(0, d)).wait_recv()
        r = pl.ds(pl.multiple_of(lax.rem(x + STEP[d], 4) * 128, 128), 128)
        x_via_out[d] = (tile[r, d * 512:d * 512 + 512] + x_far_in[d].astype(F32)).astype(BF)
        send(*x_copy(2, d))
    for kind in (1, 2):
        for d in range(2):
            copy(*x_copy(kind, d)).wait_recv()

    def chunk(step, part):
        r = pl.ds(pl.multiple_of(core * 512 + lax.rem(x + step, 4) * 128, 128), 128)
        return gram.at[r, pl.ds(part * 512, 512)]

    chunk(0, 0)[...] = (
        tile[here, 0:512] + x_via_in[0].astype(F32) + x_near_in[1].astype(F32)
    ).astype(BF)
    chunk(0, 1)[...] = (
        tile[here, 512:1024] + x_near_in[0].astype(F32) + x_via_in[1].astype(F32)
    ).astype(BF)

    def gx_copy(kind, d):
        part = d if kind in (0, 2) else 1 - d
        step = 0 if kind < 2 else STEP[1 - d]
        return chunk(step, part), chunk(step, part), gx_send.at[kind, d], gx_recv.at[kind, d], "x", d

    def gx_arrived(kind, d):
        part = d if kind in (0, 2) else 1 - d
        step = STEP[1 - d] if kind < 2 else 2
        ref = chunk(step, part)
        copy(ref, ref, gx_send.at[kind, d], gx_recv.at[kind, d], "x", d).wait_recv()
        return step, part

    def gp_copy(step, part):
        ref = chunk(step, part)
        return ref, ref, gp_send.at[step, part], gp_recv.at[step, part], "core", 0

    for kind in (0, 1):
        for d in range(2):
            send(*gx_copy(kind, d))
    for part in range(2):
        send(*gp_copy(0, part))
    sq_start(3, "core", sq_total(2, "x"))
    arrived = []
    for d in range(2):
        arrived.append(gx_arrived(0, d))
        send(*gx_copy(2, d))
    for d in range(2):
        send(*gp_copy(*arrived[d]))
    for kind in (1, 2):
        for d in range(2):
            send(*gp_copy(*gx_arrived(kind, d)))
    for step in range(4):
        for part in range(2):
            r = pl.ds(pl.multiple_of((1 - core) * 512 + lax.rem(x + step, 4) * 128, 128), 128)
            ref = gram.at[r, pl.ds(part * 512, 512)]
            copy(ref, ref, gp_send.at[step, part], gp_recv.at[step, part], "core", 0).wait_recv()

    total = jnp.sum(sq_total(3, "core")[0:1, :], axis=1, keepdims=True)
    factor = NORM_SHARE * math.sqrt(ROWS) / (jnp.sqrt(total) + NORM_EPSILON)

    def down(lhs, slot):
        return dot(lhs, gram[:, slot * 256:slot * 256 + 256])

    def across(lhs, slot):
        return dot(lhs, gram[slot * 256:slot * 256 + 256, :], NT)

    for slot in (3, 1, 2, 0):
        w = down(z_group[0:512, :], slot)
        rs_put(1, 0, "z", slot, w[0:256], w[256:512])
        w = across(y_group[512:1024, :], slot)
        rs_put(1, 1, "y", slot, w[0:256], w[256:512])
    for h in range(2):
        rs_relay(1, h, AXIS1[h])
    for h in range(2):
        for part, w in enumerate(rs_finish(1, h, AXIS1[h])):
            r = pl.ds(part * 256, 256)
            v = CUBIC_COEF * grad[h, r] + (QUINTIC_COEF * factor * factor) * w
            values[h, r, 0:256] = v.astype(BF)
            ag_own(2 + h, values.at[h], 256, AXIS1[h], part)
    for h in range(2):
        ag_relay(2 + h, values.at[h], 256, AXIS1[h])
    for h in range(2):
        ag_near(2 + h, values.at[h], 256, AXIS1[h])
        ag_far(2 + h, values.at[h], 256, AXIS1[h])
    for slot in (3, 1, 2, 0):
        m = across(values[0], slot)
        rs_put(2, 0, "y", slot, m[0:256], m[256:512])
        m = down(values[1], slot)
        rs_put(2, 1, "z", slot, m[0:256], m[256:512])
    for h in range(2):
        rs_relay(2, h, AXIS2[h])
    scale = math.sqrt(N) * factor
    for h in range(2):
        for part, m in enumerate(rs_finish(2, h, AXIS2[h])):
            r = pl.ds(part * 256, 256)
            o = scale * (LINEAR_COEF * grad[h, r] + (factor * factor) * m)
            out_ref[:, h * 512 + part * 256:h * 512 + part * 256 + 256] = o.T.astype(BF)

    def drain(k, carry):
        for h in range(2):
            for d in range(2):
                far_copy(h, d, k).wait_send()
                near_copy(h, d, k).wait_send()
                via_copy(h, d, k).wait_send()
        return carry

    lax.fori_loop(0, 4, drain, 0)
    for c in sent:
        c.wait_send()


def local(cotangent, activation):
    dma = pltpu.SemaphoreType.DMA
    vm = pltpu.VMEM
    piece = (256, 256)
    return pl.pallas_call(
        kernel,
        out_shape=jax.ShapeDtypeStruct((256, 1024), BF),
        in_specs=[pl.BlockSpec(memory_space=pl.ANY)] * 2,
        out_specs=pl.BlockSpec(memory_space=pltpu.VMEM),
        scratch_shapes=[
            vm((1024, 2048), BF), vm((16, 2048, 256), BF), dma((4,)), dma((16,)),
            vm((2, 4, 512, 256), BF), vm((2, 2, 4) + piece, BF),
            vm((2, 2, 4) + piece, BF), vm((2, 2, 4) + piece, BF),
            vm((2, 2, 4) + piece, BF), vm((2, 2, 4) + piece, BF),
            vm((1024, 1024), F32), vm((2, 4, 512, 256), F32),
            dma((3, 2, 2, 4)), dma((3, 2, 2, 4)),
            vm((3, 2, 512, 256), BF), vm((3, 2, 2) + piece, BF),
            vm((3, 2, 2) + piece, BF), vm((3, 2, 2) + piece, BF),
            vm((3, 2, 2) + piece, BF), vm((3, 2, 2) + piece, BF),
            dma((3, 2, 3, 2)), dma((3, 2, 3, 2)),
            vm((2, 512, 256), F32), vm((1024, 1024), BF), vm((1024, 1024), BF), dma((4, 3, 2)), dma((4, 3, 2)),
            vm((512, 1024), BF), dma((4,)), dma((4,)),
            vm((2, 128, 512), BF), vm((2, 128, 512), BF), vm((2, 128, 512), BF),
            vm((2, 128, 512), BF), vm((2, 128, 512), BF), vm((2, 128, 512), BF), dma((3, 2)), dma((3, 2)),
            vm((1024, 1024), BF), dma((3, 2)), dma((3, 2)), dma((4, 2)), dma((4, 2)),
            vm((2, 512, 1024), BF), vm((4, 4, 8, 256), F32), dma((4, 4)), dma((4, 4)),
        ],
        compiler_params=pltpu.CompilerParams(
            collective_id=0, has_side_effects=True, vmem_limit_bytes=67043328
        ),
        name="muon_step",
    )(cotangent, activation)


def solution(mesh):
    return jax.shard_map(
        local,
        mesh=mesh,
        in_specs=(P("dp", None), P("dp", "mp")),
        out_specs=P("dp", "mp"),
        check_vma=False,
    )
```
